32 devices in a mesh: expert: 8 (over y, x, core), tensor: 4 (over z).
Axes of the slice: x: 2, y: 2, z: 4, core: 2. Of those that a mesh axis runs over, the one named last changes fastest.
Arguments:
- tokens: bfloat16 [2560, 4096], P('expert', 'tensor'), may hold values from -6 to 6
- grad_out: bfloat16 [2560, 4096], P('expert', 'tensor'), may hold values from -6 to 6
- routes: int32 [2560, 4], P('expert'), may hold values from 0 to 7, all different within a row; in each aligned block of 320 rows (0 to 319, 320 to 639, ...) at most 200 rows name the same one
- route_weights: float32 [2560, 4], P('expert'), may hold values from 0.05 to 0.5
- swap_flags: int32 [4], replicated, may hold values from 0 to 1023
- weights: bfloat16 [8, 3, 1536, 4096], P('expert', None, None, 'tensor'), may hold values from -0.09375 to 0.09375
- first_moment: bfloat16 [8, 3, 1536, 4096], P('expert', None, None, 'tensor'), may hold values from -8 to 8
- second_moment: bfloat16 [8, 3, 1536, 4096], P('expert', None, None, 'tensor'), may hold values from 1 to 30
Outputs:
- combined: bfloat16 [2560, 4096], P('expert', 'tensor')
- update: bfloat16 [8, 3, 1536, 4096], P('expert', None, None, 'tensor')
The draws below stay inside these ranges and needn't reach their ends.
Inputs may be any that keep to these rules, and one draw needn't show every extreme that they name: `routes`: in each aligned block of 320 rows no expert is named by more than 200 rows, a bound that some block reaches; a row names 4 different experts.
All inputs are finite; a program needn't handle non-finite values.
Results may differ from the reference program's by a relative error of at most 0.023.
Values may be sent and summed in bfloat16 or wider, within the bound.
A program may use at most 192 MiB of HBM per device.

```python
import math
import jax
import jax.numpy as jnp
import numpy as np
from jax import lax

D = 4096
FF = 1536
TOK_DEV = 320
ROUTES = 4
EXPERTS = 8
TOKENS = 2560
CAP = 200
D_SHARD = 1024
N_EXPERT = 8
N_TENSOR = 4


def set_ends(values, stream_key, low, top_value):
    extent = values.shape
    place = [jax.random.randint(jax.random.fold_in(stream_key, axis), (), 0, extent[axis]) for axis in range(len(extent))]
    values = values.at[tuple(place)].set(low)
    longest = extent.index(max(extent))
    place[longest] = (place[longest] + 1) % extent[longest]
    return values.at[tuple(place)].set(top_value)


def block_scale(key, extent, split, least, top_value):
    factor_of = 1.0
    for position, blocks in split:
        draws = jax.random.uniform(jax.random.fold_in(jax.random.fold_in(key, 6), position), (blocks,), jnp.float32, least / len(split), top_value / len(split))
        factor_of = factor_of * jnp.repeat(jnp.exp(draws), extent[position] // blocks).reshape((-1,) + (1,) * (len(extent) - 1 - position))
    return factor_of


def deal_out(rng, own, number, rows, count, top, reach, skew):
    order = jax.random.permutation(rng, count)
    heavy_load, common = load_shares(count, rows * top, reach, skew, True), load_shares(count, rows * top, reach, skew, False)
    places = jnp.arange(count)

    def named(lengths, turn):
        used = int((lengths > 0).sum())
        fixed = max(1, used // 4)
        passed = fixed + (places - fixed + turn * (used - fixed)) % max(1, count - fixed)
        return jnp.zeros((count,), jnp.int32).at[order[jnp.where(places < fixed, places, passed)]].set(jnp.asarray(lengths, jnp.int32))

    lengths = jnp.where(number % 4 == 0, named(heavy_load, number // 4), named(common, number - number // 4 - 1))
    mixed = jax.random.permutation(jax.random.fold_in(own, 3), count)
    giver, taker = mixed[0:count // 2 * 2:2], mixed[1:count // 2 * 2:2]
    margin = jnp.minimum(lengths[giver] - 1, reach - lengths[taker]) // 2
    margin = jnp.where((giver == order[0]) | (taker == order[0]) | (lengths[taker] == 0), 0, jnp.maximum(margin, 0))
    passed = jax.random.randint(jax.random.fold_in(own, 4), (count // 2,), 0, 1 << 20) % (margin + 1)
    lengths = lengths.at[giver].add(-passed).at[taker].add(passed)
    labels = jnp.searchsorted(jnp.cumsum(lengths), jnp.arange(rows * top), side="right").astype(jnp.int32)
    table = labels.reshape(top, rows).T
    table = table[jax.random.permutation(jax.random.fold_in(own, 1), rows)]
    turn = jax.random.randint(jax.random.fold_in(own, 2), (rows, 1), 0, top)
    return jnp.take_along_axis(table, (jnp.arange(top)[None, :] + turn) % top, axis=1)


def load_shares(number_of, total, most, lean, full):
    loads = [(1 << 20) // math.isqrt(standing ** lean) + 1 for standing in range(1, number_of + 1)]
    largest = most if full else min(most, max(-(-total // number_of), total * loads[0] // sum(loads)))
    least = 1 if total - largest >= number_of - 1 else 0
    holding, spare = [largest] + [least] * (number_of - 1), total - largest - least * (number_of - 1)
    while spare > 0:
        movable = [i for i in range(1, number_of) if holding[i] < largest] or [i for i in range(1, number_of) if holding[i] < most]
        mass, remaining = sum([loads[i] for i in movable]), spare
        for i in movable:
            addition = min(most - holding[i], max(1, remaining * loads[i] // mass), spare)
            holding[i] = holding[i] + addition
            spare = spare - addition
    return np.array(holding)


def bell_draw(stream_key, shape, width, limit, cuts=(), kind=jnp.bfloat16):
    entries = jax.random.normal(stream_key, shape, jnp.float32) * width
    if len(cuts) > 0:
        entries = block_scale(stream_key, shape, cuts, -0.22, 0.18) * entries
    return jnp.clip(entries, min=-limit, max=limit).astype(kind)


def setup_inputs(seed: int = 0) -> dict:
    keys = jax.random.split(jax.random.key(seed), 9)
    tokens = bell_draw(keys[0], (TOKENS, D), 1.0, 6.0, ((0, 8), (1, 4)))
    grad_out = bell_draw(keys[1], (TOKENS, D), 1.0, 6.0, ((0, 8), (1, 4)))
    routes_keys = jax.random.split(jax.random.fold_in(keys[2], 1), TOKENS // TOK_DEV)
    routes_turns = jax.random.permutation(jax.random.fold_in(keys[2], 3), TOKENS // TOK_DEV)
    routes = jax.vmap(lambda own, number: deal_out(jax.random.fold_in(keys[2], 2), own, number, TOK_DEV, EXPERTS, ROUTES, CAP, 2))(routes_keys, routes_turns).reshape((TOKENS, ROUTES))
    route_weights = jnp.clip(jnp.exp(math.log(0.5) - 2.3025851 * jax.random.uniform(keys[3], (TOKENS, ROUTES), jnp.float32) ** block_scale(keys[3], (TOKENS, ROUTES), ((0, 8),), -0.2, 0.2)), 0.05, 0.5)
    swap_flags = set_ends(jax.random.randint(keys[4], (EXPERTS // 2,), 0, 1024), jax.random.fold_in(keys[4], 1), 0, 1023).astype(jnp.int32)
    weights = bell_draw(keys[5], (EXPERTS, 3, FF, D), D ** -0.5, 0.09375, ((0, 8), (3, 4)))
    first_moment = bell_draw(keys[6], (EXPERTS, 3, FF, D), 2.0, 8.0, ((0, 8), (3, 4)))
    second_moment = jnp.clip(jnp.exp(math.log(30.0) - 3.4011974 * jax.random.uniform(keys[7], (EXPERTS, 3, FF, D), jnp.float32) ** block_scale(keys[7], (EXPERTS, 3, FF, D), ((0, 8), (3, 4)), -0.2, 0.2)), 1.0, 30.0).astype(jnp.bfloat16)
    return {"tokens": tokens, "grad_out": grad_out, "routes": routes, "route_weights": route_weights, "swap_flags": swap_flags, "weights": weights, "first_moment": first_moment, "second_moment": second_moment}


correction_one = 1.0 - 0.9 ** 20
correction_two = 1.0 - 0.95 ** 20

def block_sum(left_rows, right_rows):
    left_blocks = left_rows.reshape(left_rows.shape[0], N_TENSOR, D_SHARD).astype(jnp.float32)
    right_blocks = right_rows.reshape(right_rows.shape[0], N_TENSOR, D_SHARD).astype(jnp.float32)
    partials = jnp.einsum('sjd,rjd->jsr', left_blocks, right_blocks)
    rounded = lax.optimization_barrier(partials.astype(jnp.bfloat16))
    return lax.optimization_barrier(jnp.sum(rounded.astype(jnp.float32), axis=0))

def reference(tokens, grad_out, routes, route_weights, swap_flags, weights, first_moment, second_moment):
    block_slots = TOK_DEV * ROUTES
    slot_total = TOKENS * ROUTES
    experts_range = jnp.arange(EXPERTS, dtype=jnp.int32)
    flat_ids = routes.reshape(N_EXPERT, block_slots).astype(jnp.int32)
    id_onehot = (flat_ids[:, :, None] == experts_range[None, None, :]).astype(jnp.int32)
    slot_rank = lax.optimization_barrier(jnp.sum((jnp.cumsum(id_onehot, axis=1) - id_onehot) * id_onehot, axis=2))
    group_index = jnp.arange(N_EXPERT, dtype=jnp.int32)[:, None]
    slot_index = (flat_ids * (N_EXPERT * CAP) + group_index * CAP + slot_rank).reshape(-1)
    flat_slot = jnp.arange(slot_total, dtype=jnp.int32)
    table_rows = jnp.full((EXPERTS * N_EXPERT * CAP,), slot_total, jnp.int32).at[slot_index].set(flat_slot)
    table_rows = table_rows.reshape(EXPERTS, N_EXPERT * CAP)
    token_pad = jnp.concatenate([tokens, jnp.zeros((1, D), tokens.dtype)], axis=0)
    scaled_grad = (route_weights[:, :, None] * grad_out[:, None, :].astype(jnp.float32)).astype(jnp.bfloat16)
    grad_pad = jnp.concatenate([scaled_grad.reshape(slot_total, D), jnp.zeros((1, D), jnp.bfloat16)], axis=0)

    def expert_pass(packed):
        entry_rows, expert_weight, moment_one, moment_two = packed
        token_slots = token_pad[entry_rows // ROUTES]
        grad_slots = grad_pad[entry_rows]
        preact = block_sum(token_slots, expert_weight[0:2].reshape(2 * FF, D))
        gate_pre = preact[:, :FF]
        up_pre = preact[:, FF:]
        sig_gate = jax.nn.sigmoid(gate_pre)
        hidden = (gate_pre * sig_gate * up_pre).astype(jnp.bfloat16)
        output_slots = jnp.dot(hidden, expert_weight[2], preferred_element_type=jnp.float32).astype(jnp.bfloat16)
        hidden_grad = block_sum(grad_slots, expert_weight[2])
        gate_grad = (hidden_grad * up_pre * sig_gate * (1.0 + gate_pre * (1.0 - sig_gate))).astype(jnp.bfloat16)
        up_grad = (hidden_grad * gate_pre * sig_gate).astype(jnp.bfloat16)
        weight_grad = jnp.stack([jnp.dot(gate_grad.T, token_slots, preferred_element_type=jnp.float32), jnp.dot(up_grad.T, token_slots, preferred_element_type=jnp.float32), jnp.dot(hidden.T, grad_slots, preferred_element_type=jnp.float32)])
        moment_new = 0.9 * moment_one.astype(jnp.float32) + 0.1 * weight_grad
        square_new = 0.95 * moment_two.astype(jnp.float32) + 0.05 * weight_grad * weight_grad
        step_dir = moment_new / correction_one / (jnp.sqrt(square_new / correction_two) + 1e-08)
        return (step_dir.astype(jnp.bfloat16), output_slots)
    step_all, output_all = lax.map(expert_pass, (table_rows, weights, first_moment, second_moment))
    gathered_out = output_all.reshape(EXPERTS * N_EXPERT * CAP, D)[slot_index]
    gathered_out = gathered_out.reshape(TOKENS, ROUTES, D).astype(jnp.float32)
    combined = lax.optimization_barrier(jnp.sum(route_weights[:, :, None] * gathered_out, axis=1)).astype(jnp.bfloat16)
    paired = jnp.repeat(jnp.bitwise_and(swap_flags.astype(jnp.int32), 1), 2)
    held_expert = jnp.where(paired == 1, jnp.bitwise_xor(experts_range, 1), experts_range)
    update = jnp.take(step_all, held_expert, axis=0)
    return (combined, update)
```

```python
import functools
import jax
import jax.numpy as jnp
from jax import lax
from jax.experimental import pallas as pl
from jax.experimental.pallas import tpu as pltpu
from jax.sharding import PartitionSpec as P

MESH = pl.DeviceIdType.MESH
COLS = 128
SUB = 4
LAG = 2
ONE = 1.0 / (1.0 - 0.9**20)
TWO = 1.0 / (1.0 - 0.95**20)


def contract_last(left_rows, right_rows):
    return lax.dot_general(
        left_rows, right_rows, (((1,), (1,)), ((), ())), preferred_element_type=jnp.float32
    )


def contract_first(left_rows, right_rows):
    return lax.dot_general(
        left_rows, right_rows, (((0,), (0,)), ((), ())), preferred_element_type=jnp.float32
    )


def flip(spot, other, count):
    total, bit = 0, 1
    while bit < count:
        total = total + bit * lax.rem(lax.div(spot, bit) + lax.div(other, bit), 2)
        bit *= 2
    return total


def kernel(
    groups, line, ring, passes,
    tokens, grads, routes, route_w, trade, weights, first, second,
    combined, update,
    counted, ranks, shares, masks, xs, gs, send_x, send_g, returned, out_sum, wv, total,
    own, came, moment, square, mine, theirs, comb,
    x_send, x_recv, g_send, g_recv, o_send, o_recv,
    in_send, in_recv, out_send, w_sem, m_sem, u_send, u_recv, u_out,
):
    toks, width = tokens.shape
    rows = xs.shape[1]
    units = passes * groups * SUB
    blocks = passes * SUB
    half = line // 2
    inner = half - 1
    me = lax.axis_index("expert")
    spot = lax.axis_index("tensor")
    near = (spot < half).astype(jnp.int32)
    depth = near * spot + (1 - near) * (line - 1 - spot)
    inward = spot + 2 * near - 1
    outward = spot + 1 - 2 * near
    is_mid = (depth == inner).astype(jnp.int32)
    lag_total = LAG * (half + inner - depth)
    partner = flip(me, jnp.int32(1), groups)

    def w_copy(m):
        return pltpu.make_async_copy(
            weights.at[0, :, pl.ds(m * COLS, COLS), :], wv.at[m], w_sem.at[m]
        )

    def m_copies(m):
        k = lax.rem(m, 2)
        cut = pl.ds(pl.multiple_of(m * COLS, COLS), COLS)
        return (
            pltpu.make_async_copy(first.at[0, :, cut, :], moment.at[k], m_sem.at[0, k]),
            pltpu.make_async_copy(second.at[0, :, cut, :], square.at[k], m_sem.at[1, k]),
        )

    def x_copy(j):
        return pltpu.make_async_remote_copy(
            send_x.at[j], xs.at[j], x_send.at[j], x_recv.at[j],
            device_id={"expert": flip(me, j, groups)}, device_id_type=MESH,
        )

    def g_copy(j):
        return pltpu.make_async_remote_copy(
            send_g.at[j], gs.at[j], g_send.at[j], g_recv.at[j],
            device_id={"expert": flip(me, j, groups)}, device_id_type=MESH,
        )

    def o_copy(j):
        return pltpu.make_async_remote_copy(
            send_x.at[j], returned.at[j], o_send.at[j], o_recv.at[j],
            device_id={"expert": flip(me, j, groups)}, device_id_type=MESH,
        )

    def in_copy(slot):
        return pltpu.make_async_remote_copy(
            own.at[slot], came.at[is_mid, slot], in_send.at[slot], in_recv.at[is_mid, slot],
            device_id={"tensor": inward}, device_id_type=MESH,
        )

    def out_copy(slot):
        return pltpu.make_async_remote_copy(
            came.at[1, slot], came.at[1, slot], out_send.at[slot], in_recv.at[1, slot],
            device_id={"tensor": outward}, device_id_type=MESH,
        )

    def arrived(kind, slot):
        pltpu.make_async_remote_copy(
            own.at[slot], came.at[kind, slot], in_send.at[slot], in_recv.at[kind, slot],
            device_id={"tensor": inward}, device_id_type=MESH,
        ).wait_recv()

    def u_copy(k):
        return pltpu.make_async_remote_copy(
            mine.at[k], theirs.at[k], u_send.at[k], u_recv.at[k],
            device_id={"expert": partner}, device_id_type=MESH,
        )

    def u_store(m):
        k = lax.rem(m, 2)
        cut = pl.ds(pl.multiple_of(m * COLS, COLS), COLS)
        return pltpu.make_async_copy(mine.at[k], update.at[0, :, cut, :], u_out.at[k])

    for m in range(blocks):
        w_copy(m).start()
    for m in range(2):
        for copy in m_copies(m):
            copy.start()

    lane = lax.broadcasted_iota(jnp.int32, (toks, 128), 1)
    hits = jnp.zeros((toks, 128), jnp.float32)
    share = jnp.zeros((toks, 128), jnp.float32)
    for r in range(routes.shape[1]):
        hit = routes[:, r : r + 1] == lane
        hits = hits + jnp.where(hit, 1.0, 0.0)
        share = share + jnp.where(hit, route_w[:, r : r + 1], 0.0)
    counted[...] = hits
    shares[...] = share
    later = lax.broadcasted_iota(jnp.int32, (toks, toks), 0)
    sooner = lax.broadcasted_iota(jnp.int32, (toks, toks), 1)
    below = jnp.where(sooner < later, 1.0, 0.0).astype(jnp.bfloat16)
    ranks[...] = jnp.dot(below, hits.astype(jnp.bfloat16), preferred_element_type=jnp.float32)

    def column(table, expert):
        return jnp.sum(jnp.where(lane == expert, table[...], 0.0), axis=1, keepdims=True)

    def dispatch(j):
        expert = flip(me, j, groups)
        place = jnp.where(column(counted, expert) > 0.5, column(ranks, expert), -1.0)
        slot = lax.broadcasted_iota(jnp.int32, (toks, rows), 1)
        mask = jnp.where(place.astype(jnp.int32) == slot, 1.0, 0.0).astype(jnp.bfloat16)
        masks[j] = mask
        scaled = (column(shares, expert) * grads[...].astype(jnp.float32)).astype(jnp.bfloat16)
        picked = contract_first(mask, tokens[...]).astype(jnp.bfloat16)
        scaled_picked = contract_first(mask, scaled).astype(jnp.bfloat16)

        @pl.when(j == 0)
        def _():
            xs[0] = picked
            gs[0] = scaled_picked

        @pl.when(j > 0)
        def _():
            send_x[j] = picked
            send_g[j] = scaled_picked
            x_copy(j).start()
            g_copy(j).start()

    def split(u):
        span = groups * SUB
        big = lax.div(u, span)
        rest = lax.rem(u, span)
        place = lax.div(rest, SUB)
        turn = (big == passes - 1).astype(jnp.int32)
        return big, place, place + turn * (groups - 1 - 2 * place), lax.rem(rest, SUB)

    def settle(m):
        k = lax.rem(m, 2)
        u_copy(k).wait()
        swap = trade[...] > 0

        def piece(s, _):
            cut = pl.ds(pl.multiple_of(s * 16, 16), 16)
            for q in range(3):
                kept = mine[k, q, cut, :].astype(jnp.float32)
                moved = theirs[k, q, cut, :].astype(jnp.float32)
                mine[k, q, cut, :] = jnp.where(swap, moved, kept).astype(jnp.bfloat16)
            return 0

        lax.fori_loop(0, COLS // 16, piece, 0)
        u_store(m).start()

    def adam(m, b):
        k = lax.rem(m, 2)

        @pl.when(m > 0)
        def _():
            settle(m - 1)

        @pl.when(m > 1)
        def _():
            u_store(m - 2).wait()

        for copy in m_copies(m):
            copy.wait()

        def piece(s, _):
            cut = pl.ds(pl.multiple_of(s * 16, 16), 16)
            for q in range(3):
                grad = total[b, q, cut, :]
                moment_new = 0.9 * moment[k, q, cut, :].astype(jnp.float32) + 0.1 * grad
                square_new = 0.95 * square[k, q, cut, :].astype(jnp.float32) + 0.05 * grad * grad
                step = moment_new * ONE / (jnp.sqrt(square_new * TWO) + 1e-08)
                mine[k, q, cut, :] = step.astype(jnp.bfloat16)
            return 0

        lax.fori_loop(0, COLS // 16, piece, 0)
        u_copy(k).start()

        @pl.when(m + 2 < blocks)
        def _():
            for copy in m_copies(m + 2):
                copy.start()

    def start_unit(u):
        big, place, j, b = split(u)
        slot = lax.rem(u, ring)
        m = big * SUB + b

        @pl.when((big == 0) & (b == 0) & (j > 0))
        def _():
            x_copy(j).wait_recv()
            g_copy(j).wait_recv()

        @pl.when(place == 0)
        def _():
            w_copy(m).wait()

        @pl.when(u >= ring)
        def _():
            in_copy(slot).wait_send()

        both = contract_last(xs[j], wv[m, 0:2].reshape(2 * COLS, width))
        own[slot, :, 0 : 2 * COLS] = both.astype(jnp.bfloat16)
        own[slot, :, 2 * COLS :] = contract_last(gs[j], wv[m, 2]).astype(jnp.bfloat16)

        @pl.when(depth == 0)
        def _():
            in_copy(slot).start()

    def pass_unit(u):
        slot = lax.rem(u, ring)
        arrived(0, slot)
        own[slot] = (
            own[slot].astype(jnp.float32) + came[0, slot].astype(jnp.float32)
        ).astype(jnp.bfloat16)
        in_copy(slot).start()

    def finish_unit(u):
        big, place, j, b = split(u)
        slot = lax.rem(u, ring)
        m = big * SUB + b
        arrived(1, slot)

        @pl.when(depth == inner)
        def _():
            came[1, slot] = (
                own[slot].astype(jnp.float32) + came[1, slot].astype(jnp.float32)
            ).astype(jnp.bfloat16)

        @pl.when(depth > 0)
        def _():
            @pl.when(u >= 2)
            def _():
                out_copy(lax.rem(u - 2, ring)).wait_send()

            out_copy(slot).start()

        gate = came[1, slot, :, 0:COLS].astype(jnp.float32)
        up = came[1, slot, :, COLS : 2 * COLS].astype(jnp.float32)
        back = came[1, slot, :, 2 * COLS :].astype(jnp.float32)
        sig = jax.nn.sigmoid(gate)
        hidden = (gate * sig * up).astype(jnp.bfloat16)
        gate_grad = (back * up * sig * (1.0 + gate * (1.0 - sig))).astype(jnp.bfloat16)
        up_grad = (back * gate * sig).astype(jnp.bfloat16)
        out = jnp.dot(hidden, wv[m, 2], preferred_element_type=jnp.float32)

        @pl.when(m == 0)
        def _():
            out_sum[j] = out

        @pl.when(m > 0)
        def _():
            out_sum[j] += out

        pair = jnp.concatenate([gate_grad, up_grad], axis=1)
        pair_sum = contract_first(pair, xs[j]).reshape(2, COLS, width)
        down_sum = contract_first(hidden, gs[j])

        @pl.when(place == 0)
        def _():
            total[b, 0:2] = pair_sum
            total[b, 2] = down_sum

        @pl.when(place > 0)
        def _():
            total[b, 0:2] += pair_sum
            total[b, 2] += down_sum

        @pl.when(m == blocks - 1)
        def _():
            @pl.when(j > 0)
            def _():
                x_copy(j).wait_send()
                send_x[j] = out_sum[j].astype(jnp.bfloat16)
                o_copy(j).start()

            @pl.when(j == 0)
            def _():
                returned[0] = out_sum[0].astype(jnp.bfloat16)

        @pl.when(place == groups - 1)
        def _():
            adam(m, b)

    def step(i, _):
        @pl.when(i < groups)
        def _():
            dispatch(i)

        @pl.when(i < units)
        def _():
            start_unit(i)

        @pl.when((depth > 0) & (i >= LAG * depth) & (i - LAG * depth < units))
        def _():
            pass_unit(i - LAG * depth)

        @pl.when((i >= lag_total) & (i - lag_total < units))
        def _():
            finish_unit(i - lag_total)

        return 0

    lax.fori_loop(0, units + LAG * (line - 1), step, 0)

    comb[...] = jnp.zeros_like(comb)

    def gather(place, _):
        j = groups - 1 - place

        @pl.when(j > 0)
        def _():
            o_copy(j).wait()
            g_copy(j).wait_send()

        expert = flip(me, j, groups)
        rows_back = jnp.dot(masks[j], returned[j], preferred_element_type=jnp.float32)
        comb[...] += column(shares, expert) * rows_back
        return 0

    lax.fori_loop(0, groups, gather, 0)
    combined[...] = comb[...].astype(jnp.bfloat16)

    settle(blocks - 1)
    for m in (blocks - 2, blocks - 1):
        u_store(m).wait()
    for back in range(min(ring, units)):
        in_copy((units - 1 - back) % ring).wait_send()

    @pl.when(depth > 0)
    def _():
        for u in (units - 2, units - 1):
            out_copy(u % ring).wait_send()


def body(tokens, grad_out, routes, route_weights, swap_flags, weights, first_moment, second_moment):
    groups, line = lax.axis_size("expert"), lax.axis_size("tensor")
    toks, width = tokens.shape
    hidden_width = weights.shape[2]
    cap = toks * routes.shape[1] * 5 // (4 * groups)
    rows = -(-cap // 16) * 16
    passes = hidden_width // (COLS * SUB)
    blocks = passes * SUB
    ring = LAG * (line - 1) + 3
    me = lax.axis_index("expert")
    paired = jnp.repeat(jnp.bitwise_and(swap_flags, 1), 2)
    traded = jnp.sum(jnp.where(jnp.arange(groups) == me, paired, 0))
    trade = jnp.broadcast_to(traded.astype(jnp.int32), (16, width))
    bf, f32 = jnp.bfloat16, jnp.float32
    dma = pltpu.SemaphoreType.DMA
    whole = pl.BlockSpec(memory_space=pltpu.VMEM)
    left = pl.BlockSpec(memory_space=pl.ANY)
    flops = 2 * groups * rows * width * hidden_width * 7
    combined, update = pl.pallas_call(
        functools.partial(kernel, groups, line, ring, passes),
        out_shape=(
            jax.ShapeDtypeStruct((toks, width), bf),
            jax.ShapeDtypeStruct(weights.shape, bf),
        ),
        in_specs=[whole] * 5 + [left] * 3,
        out_specs=(whole, left),
        scratch_shapes=[
            pltpu.VMEM((toks, 128), f32),
            pltpu.VMEM((toks, 128), f32),
            pltpu.VMEM((toks, 128), f32),
            pltpu.VMEM((groups, toks, rows), bf),
            pltpu.VMEM((groups, rows, width), bf),
            pltpu.VMEM((groups, rows, width), bf),
            pltpu.VMEM((groups, rows, width), bf),
            pltpu.VMEM((groups, rows, width), bf),
            pltpu.VMEM((groups, rows, width), bf),
            pltpu.VMEM((groups, rows, width), f32),
            pltpu.VMEM((blocks, 3, COLS, width), bf),
            pltpu.VMEM((SUB, 3, COLS, width), f32),
            pltpu.VMEM((ring, rows, 3 * COLS), bf),
            pltpu.VMEM((2, ring, rows, 3 * COLS), bf),
            pltpu.VMEM((2, 3, COLS, width), bf),
            pltpu.VMEM((2, 3, COLS, width), bf),
            pltpu.VMEM((2, 3, COLS, width), bf),
            pltpu.VMEM((2, 3, COLS, width), bf),
            pltpu.VMEM((toks, width), f32),
            dma((groups,)), dma((groups,)), dma((groups,)), dma((groups,)),
            dma((groups,)), dma((groups,)),
            dma((ring,)), dma((2, ring)), dma((ring,)),
            dma((blocks,)), dma((2, 2)), dma((2,)), dma((2,)), dma((2,)),
        ],
        compiler_params=pltpu.CompilerParams(
            has_side_effects=True, vmem_limit_bytes=66_000_000
        ),
        cost_estimate=pl.CostEstimate(
            flops=flops, bytes_accessed=8 * weights.size, transcendentals=0
        ),
    )(tokens, grad_out, routes, route_weights, trade, weights, first_moment, second_moment)
    return combined, update


def solution(mesh):
    placed = (
        P("expert", "tensor"),
        P("expert", "tensor"),
        P("expert", None),
        P("expert", None),
        P(),
        P("expert", None, None, "tensor"),
        P("expert", None, None, "tensor"),
        P("expert", None, None, "tensor"),
    )
    return jax.shard_map(
        body,
        mesh=mesh,
        in_specs=placed,
        out_specs=(P("expert", "tensor"), P("expert", None, None, "tensor")),
        check_vma=False,
    )
```

```python
import functools
import jax
import jax.numpy as jnp
from jax import lax
from jax.experimental import pallas as pl
from jax.experimental.pallas import tpu as pltpu
from jax.sharding import PartitionSpec as P

MESH = pl.DeviceIdType.MESH
COLS = 128
SUB = 6
LAG = 2
ONE = 1.0 / (1.0 - 0.9**20)
TWO = 1.0 / (1.0 - 0.95**20)


def contract_last(left_rows, right_rows):
    return lax.dot_general(
        left_rows, right_rows, (((1,), (1,)), ((), ())), preferred_element_type=jnp.float32
    )


def contract_first(left_rows, right_rows):
    return lax.dot_general(
        left_rows, right_rows, (((0,), (0,)), ((), ())), preferred_element_type=jnp.float32
    )


def flip(spot, other, count):
    total, bit = 0, 1
    while bit < count:
        total = total + bit * lax.rem(lax.div(spot, bit) + lax.div(other, bit), 2)
        bit *= 2
    return total


def kernel(
    groups, line, ring, passes, cap,
    tokens, grads, routes, route_w, weights, first, second,
    combined, both_steps,
    counted, ranks, shares, masks, xs, gs, send_x, send_g, returned, out_sum, wv, total,
    own, came, moment, square, mine, comb,
    x_send, x_recv, g_send, g_recv, o_send, o_recv,
    in_send, in_recv, out_send, w_sem, m_sem, u_send, u_recv, u_out,
):
    toks, width = tokens.shape
    rows = xs.shape[1]
    units = passes * groups * SUB
    blocks = passes * SUB
    half = line // 2
    inner = half - 1
    me = lax.axis_index("expert")
    spot = lax.axis_index("tensor")
    near = (spot < half).astype(jnp.int32)
    depth = near * spot + (1 - near) * (line - 1 - spot)
    inward = spot + 2 * near - 1
    outward = spot + 1 - 2 * near
    is_mid = (depth == inner).astype(jnp.int32)
    lag_total = LAG * (half + inner - depth)
    filled = pl.ds(0, -(-cap // 8) * 8)
    partner = flip(me, jnp.int32(1), groups)

    def w_copy(m):
        return pltpu.make_async_copy(
            weights.at[0, :, pl.ds(m * COLS, COLS), :], wv.at[m], w_sem.at[m]
        )

    def m_copies(m):
        k = lax.rem(m, 2)
        cut = pl.ds(pl.multiple_of(m * COLS, COLS), COLS)
        return (
            pltpu.make_async_copy(first.at[0, :, cut, :], moment.at[k], m_sem.at[0, k]),
            pltpu.make_async_copy(second.at[0, :, cut, :], square.at[k], m_sem.at[1, k]),
        )

    def x_copy(j):
        return pltpu.make_async_remote_copy(
            send_x.at[j], xs.at[j], x_send.at[j], x_recv.at[j],
            device_id={"expert": flip(me, j, groups)}, device_id_type=MESH,
        )

    def g_copy(j):
        return pltpu.make_async_remote_copy(
            send_g.at[j], gs.at[j], g_send.at[j], g_recv.at[j],
            device_id={"expert": flip(me, j, groups)}, device_id_type=MESH,
        )

    def o_copy(j):
        return pltpu.make_async_remote_copy(
            send_x.at[j], returned.at[j], o_send.at[j], o_recv.at[j],
            device_id={"expert": flip(me, j, groups)}, device_id_type=MESH,
        )

    def in_copy(slot):
        return pltpu.make_async_remote_copy(
            own.at[slot, filled], came.at[is_mid, slot, filled], in_send.at[slot], in_recv.at[is_mid, slot],
            device_id={"tensor": inward}, device_id_type=MESH,
        )

    def out_copy(slot):
        return pltpu.make_async_remote_copy(
            came.at[1, slot, filled], came.at[1, slot, filled], out_send.at[slot], in_recv.at[1, slot],
            device_id={"tensor": outward}, device_id_type=MESH,
        )

    def arrived(kind, slot):
        pltpu.make_async_remote_copy(
            own.at[slot, filled], came.at[kind, slot, filled], in_send.at[slot], in_recv.at[kind, slot],
            device_id={"tensor": inward}, device_id_type=MESH,
        ).wait_recv()

    def u_copies(m):
        k = lax.rem(m, 2)
        cut = pl.ds(pl.multiple_of(m * COLS, COLS), COLS)
        return (
            pltpu.make_async_copy(mine.at[k], both_steps.at[0, :, cut, :], u_out.at[k]),
            pltpu.make_async_remote_copy(
                mine.at[k], both_steps.at[1, :, cut, :], u_send.at[k], u_recv.at[m],
                device_id={"expert": partner}, device_id_type=MESH,
            ),
        )

    comb[...] = jnp.zeros_like(comb)
    for m in range(blocks):
        w_copy(m).start()
    for m in range(2):
        for copy in m_copies(m):
            copy.start()

    lane = lax.broadcasted_iota(jnp.int32, (128, toks), 0)
    hits = jnp.zeros((128, toks), jnp.float32)
    share = jnp.zeros((128, toks), jnp.float32)
    for r in range(routes.shape[0]):
        hit = routes[r : r + 1, :] == lane
        hits = hits + jnp.where(hit, 1.0, 0.0)
        share = share + jnp.where(hit, route_w[r : r + 1, :], 0.0)
    later = lax.broadcasted_iota(jnp.int32, (toks, toks), 0)
    sooner = lax.broadcasted_iota(jnp.int32, (toks, toks), 1)
    same = jnp.where(sooner == later, 1.0, 0.0)
    below = jnp.where(sooner < later, 1.0, 0.0)
    counted[...] = contract_last(same.astype(jnp.bfloat16), hits.astype(jnp.bfloat16))
    ranks[...] = contract_last(below.astype(jnp.bfloat16), hits.astype(jnp.bfloat16))
    shares[...] = lax.dot_general(
        same, share, (((1,), (1,)), ((), ())),
        precision=lax.Precision.HIGHEST, preferred_element_type=jnp.float32,
    )

    def column(table, expert):
        across = lax.broadcasted_iota(jnp.int32, (toks, 128), 1)
        return jnp.sum(jnp.where(across == expert, table[...], 0.0), axis=1, keepdims=True)

    def dispatch(j):
        expert = flip(me, j, groups)
        place = jnp.where(column(counted, expert) > 0.5, column(ranks, expert), -1.0)
        slot = lax.broadcasted_iota(jnp.int32, (toks, rows), 1)
        mask = jnp.where(place.astype(jnp.int32) == slot, 1.0, 0.0).astype(jnp.bfloat16)
        masks[j] = mask
        scaled = (column(shares, expert) * grads[...].astype(jnp.float32)).astype(jnp.bfloat16)
        picked = contract_first(mask, tokens[...]).astype(jnp.bfloat16)
        scaled_picked = contract_first(mask, scaled).astype(jnp.bfloat16)

        @pl.when(j == 0)
        def _():
            xs[0] = picked
            gs[0] = scaled_picked

        @pl.when(j > 0)
        def _():
            send_x[j] = picked
            send_g[j] = scaled_picked
            x_copy(j).start()
            g_copy(j).start()

    def split(u):
        span = groups * SUB
        big = lax.div(u, span)
        rest = lax.rem(u, span)
        place = lax.div(rest, SUB)
        turn = (big == passes - 1).astype(jnp.int32)
        return big, place, place + turn * (groups - 1 - 2 * place), lax.rem(rest, SUB)

    def adam(m, b):
        k = lax.rem(m, 2)

        @pl.when(m > 1)
        def _():
            keep, give = u_copies(m - 2)
            keep.wait()
            give.wait_send()

        for copy in m_copies(m):
            copy.wait()

        def piece(s, _):
            cut = pl.ds(pl.multiple_of(s * 16, 16), 16)
            for q in range(3):
                grad = total[b, q, cut, :]
                moment_new = 0.9 * moment[k, q, cut, :].astype(jnp.float32) + 0.1 * grad
                square_new = 0.95 * square[k, q, cut, :].astype(jnp.float32) + 0.05 * grad * grad
                step = moment_new * ONE / (jnp.sqrt(square_new * TWO) + 1e-08)
                mine[k, q, cut, :] = step.astype(jnp.bfloat16)
            return 0

        lax.fori_loop(0, COLS // 16, piece, 0)
        for copy in u_copies(m):
            copy.start()

        @pl.when(m + 2 < blocks)
        def _():
            for copy in m_copies(m + 2):
                copy.start()

    def gather(place):
        j = groups - 1 - place

        @pl.when(j > 0)
        def _():
            o_copy(j).wait()
            g_copy(j).wait_send()

        expert = flip(me, j, groups)
        rows_back = jnp.dot(masks[j], returned[j], preferred_element_type=jnp.float32)
        comb[...] += column(shares, expert) * rows_back

    def start_unit(u):
        big, place, j, b = split(u)
        slot = lax.rem(u, ring)
        m = big * SUB + b

        @pl.when((big == 0) & (b == 0) & (j > 0))
        def _():
            x_copy(j).wait_recv()
            g_copy(j).wait_recv()

        @pl.when(place == 0)
        def _():
            w_copy(m).wait()

        @pl.when(u >= ring)
        def _():
            in_copy(slot).wait_send()

        both = contract_last(xs[j], wv[m, 0:2].reshape(2 * COLS, width))
        own[slot, :, 0 : 2 * COLS] = both.astype(jnp.bfloat16)
        own[slot, :, 2 * COLS :] = contract_last(gs[j], wv[m, 2]).astype(jnp.bfloat16)

        @pl.when(depth == 0)
        def _():
            in_copy(slot).start()

    def pass_unit(u):
        slot = lax.rem(u, ring)
        arrived(0, slot)
        own[slot] = (
            own[slot].astype(jnp.float32) + came[0, slot].astype(jnp.float32)
        ).astype(jnp.bfloat16)
        in_copy(slot).start()

    def finish_unit(u):
        big, place, j, b = split(u)
        slot = lax.rem(u, ring)
        m = big * SUB + b
        arrived(1, slot)

        @pl.when(depth == inner)
        def _():
            came[1, slot] = (
                own[slot].astype(jnp.float32) + came[1, slot].astype(jnp.float32)
            ).astype(jnp.bfloat16)

        @pl.when(depth > 0)
        def _():
            @pl.when(u >= 2)
            def _():
                out_copy(lax.rem(u - 2, ring)).wait_send()

            out_copy(slot).start()

        real = lax.broadcasted_iota(jnp.int32, (rows, COLS), 0) < cap

        def part(q):
            cut = slice(q * COLS, (q + 1) * COLS)
            return jnp.where(real, came[1, slot, :, cut].astype(jnp.float32), 0.0)

        gate, up, back = part(0), part(1), part(2)
        sig = jax.nn.sigmoid(gate)
        hidden = (gate * sig * up).astype(jnp.bfloat16)
        gate_grad = (back * up * sig * (1.0 + gate * (1.0 - sig))).astype(jnp.bfloat16)
        up_grad = (back * gate * sig).astype(jnp.bfloat16)
        out = jnp.dot(hidden, wv[m, 2], preferred_element_type=jnp.float32)

        @pl.when(m == 0)
        def _():
            out_sum[j] = out

        @pl.when(m > 0)
        def _():
            out_sum[j] += out

        pair = jnp.concatenate([gate_grad, up_grad], axis=1)
        pair_sum = contract_first(pair, xs[j]).reshape(2, COLS, width)
        down_sum = contract_first(hidden, gs[j])

        @pl.when(place == 0)
        def _():
            total[b, 0:2] = pair_sum
            total[b, 2] = down_sum

        @pl.when(place > 0)
        def _():
            total[b, 0:2] += pair_sum
            total[b, 2] += down_sum

        @pl.when(m == blocks - 1)
        def _():
            @pl.when(j > 0)
            def _():
                x_copy(j).wait_send()
                send_x[j] = out_sum[j].astype(jnp.bfloat16)
                o_copy(j).start()

            @pl.when(j == 0)
            def _():
                returned[0] = out_sum[0].astype(jnp.bfloat16)

        @pl.when(place == groups - 1)
        def _():
            adam(m, b)

        @pl.when((big == passes - 1) & (b == SUB // 2) & (place >= 2))
        def _():
            gather(place - 2)

    def step(i, _):
        @pl.when(i < groups)
        def _():
            dispatch(i)

        @pl.when(i < units)
        def _():
            start_unit(i)

        @pl.when((depth > 0) & (i >= LAG * depth) & (i - LAG * depth < units))
        def _():
            pass_unit(i - LAG * depth)

        @pl.when((i >= lag_total) & (i - lag_total < units))
        def _():
            finish_unit(i - lag_total)

        return 0

    lax.fori_loop(0, units + LAG * (line - 1), step, 0)

    for place in range(groups - min(groups, 2), groups):
        gather(jnp.int32(place))
    combined[...] = comb[...].astype(jnp.bfloat16)

    for m in (blocks - 2, blocks - 1):
        keep, give = u_copies(jnp.int32(m))
        keep.wait()
        give.wait_send()
    for m in range(blocks):
        u_copies(jnp.int32(m))[1].wait_recv()
    for back in range(min(ring, units)):
        in_copy((units - 1 - back) % ring).wait_send()

    @pl.when(depth > 0)
    def _():
        for u in (units - 2, units - 1):
            out_copy(u % ring).wait_send()


def pick(parts, flags, combined, both_steps, out, update, held, c_sem, in_sem, out_sem):
    rung = lax.div(lax.axis_index("expert"), 2)
    side = lax.rem(flags[rung], 2)
    span = update.shape[2] // parts
    to_out = pltpu.make_async_copy(combined, out, c_sem)
    to_out.start()

    def cut(p):
        return pl.ds(p * span, span)

    def fetch(p):
        return pltpu.make_async_copy(both_steps.at[side, :, cut(p), :], held.at[p], in_sem.at[p])

    def store(p):
        return pltpu.make_async_copy(held.at[p], update.at[0, :, cut(p), :], out_sem.at[p])

    for p in range(parts):
        fetch(p).start()
    for p in range(parts):
        fetch(p).wait()
        store(p).start()
    for p in range(parts):
        store(p).wait()
    to_out.wait()


def body(tokens, grad_out, routes, route_weights, swap_flags, weights, first_moment, second_moment):
    groups, line = lax.axis_size("expert"), lax.axis_size("tensor")
    toks, width = tokens.shape
    hidden_width = weights.shape[2]
    cap = toks * routes.shape[1] * 5 // (4 * groups)
    rows = -(-cap // 16) * 16
    passes = hidden_width // (COLS * SUB)
    blocks = passes * SUB
    ring = max(LAG * (line - 1) + 3, 2 * LAG + 5)
    bf, f32 = jnp.bfloat16, jnp.float32
    dma = pltpu.SemaphoreType.DMA
    whole = pl.BlockSpec(memory_space=pltpu.VMEM)
    left = pl.BlockSpec(memory_space=pl.ANY)
    flops = 2 * groups * rows * width * hidden_width * 7
    combined, both_steps = pl.pallas_call(
        functools.partial(kernel, groups, line, ring, passes, cap),
        out_shape=(
            jax.ShapeDtypeStruct((toks, width), bf),
            jax.ShapeDtypeStruct((2,) + weights.shape[1:], bf),
        ),
        in_specs=[whole] * 4 + [left] * 3,
        out_specs=(whole, left),
        scratch_shapes=[
            pltpu.VMEM((toks, 128), f32),
            pltpu.VMEM((toks, 128), f32),
            pltpu.VMEM((toks, 128), f32),
            pltpu.VMEM((groups, toks, rows), bf),
            pltpu.VMEM((groups, rows, width), bf),
            pltpu.VMEM((groups, rows, width), bf),
            pltpu.VMEM((groups, rows, width), bf),
            pltpu.VMEM((groups, rows, width), bf),
            pltpu.VMEM((groups, rows, width), bf),
            pltpu.VMEM((groups, rows, width), f32),
            pltpu.VMEM((blocks, 3, COLS, width), bf),
            pltpu.VMEM((SUB, 3, COLS, width), f32),
            pltpu.VMEM((ring, rows, 3 * COLS), bf),
            pltpu.VMEM((2, ring, rows, 3 * COLS), bf),
            pltpu.VMEM((2, 3, COLS, width), bf),
            pltpu.VMEM((2, 3, COLS, width), bf),
            pltpu.VMEM((2, 3, COLS, width), bf),
            pltpu.VMEM((toks, width), f32),
            dma((groups,)), dma((groups,)), dma((groups,)), dma((groups,)),
            dma((groups,)), dma((groups,)),
            dma((ring,)), dma((2, ring)), dma((ring,)),
            dma((blocks,)), dma((2, 2)), dma((2,)), dma((blocks,)), dma((2,)),
        ],
        compiler_params=pltpu.CompilerParams(
            has_side_effects=True, vmem_limit_bytes=66_000_000
        ),
        cost_estimate=pl.CostEstimate(
            flops=flops, bytes_accessed=8 * weights.size, transcendentals=0
        ),
    )(tokens, grad_out, routes.T, route_weights.T, weights, first_moment, second_moment)
    parts = 6
    return pl.pallas_call(
        functools.partial(pick, parts),
        out_shape=(
            jax.ShapeDtypeStruct((toks, width), bf),
            jax.ShapeDtypeStruct(weights.shape, bf),
        ),
        in_specs=[pl.BlockSpec(memory_space=pltpu.SMEM), whole, left],
        out_specs=(left, left),
        scratch_shapes=[
            pltpu.VMEM((parts, 3, hidden_width // parts, width), bf),
            dma, dma((parts,)), dma((parts,)),
        ],
        compiler_params=pltpu.CompilerParams(vmem_limit_bytes=66_000_000),
    )(swap_flags, combined, both_steps)


def solution(mesh):
    placed = (
        P("expert", "tensor"),
        P("expert", "tensor"),
        P("expert", None),
        P("expert", None),
        P(),
        P("expert", None, None, "tensor"),
        P("expert", None, None, "tensor"),
        P("expert", None, None, "tensor"),
    )
    return jax.shard_map(
        body,
        mesh=mesh,
        in_specs=placed,
        out_specs=(P("expert", "tensor"), P("expert", None, None, "tensor")),
        check_vma=False,
    )
```
